32 devices in a mesh: sample: 2 (over core), sx: 4 (over y, x), sy: 4 (over z).
Axes of the slice: x: 2, y: 2, z: 4, core: 2. Of those that a mesh axis runs over, the one named last changes fastest.
Arguments:
- features: bfloat16 [16, 4, 16, 32, 256], P('sx', 'sample', 'sy'), may hold values from -6 to 6
- kernel: bfloat16 [3, 3, 3, 256, 256], P(None, None, None, 'sx', 'sy'), may hold values from -0.078125 to 0.078125
- filter_bias: bfloat16 [256], P('sy'), may hold values from -3 to 3
- cotangent: bfloat16 [16, 4, 16, 32, 256], P('sx', 'sample', None, None, 'sy'), may hold values from -6 to 6
Outputs:
- output: bfloat16 [16, 4, 16, 32, 256], P('sx', 'sample', None, None, 'sy')
- input_grad: bfloat16 [16, 4, 16, 32, 256], P('sx', 'sample', 'sy')
- kernel_grad: float32 [3, 3, 3, 256, 256], P(None, None, None, 'sx', 'sy')
The draws below stay inside these ranges and needn't reach their ends.
All inputs are finite; a program needn't handle non-finite values.
Results may differ from the reference program's by a relative error of at most 0.014.
Values may be sent and summed in bfloat16 or wider, within the bound.
A program may use at most 128 MiB of HBM per device.

```python
import jax
import jax.numpy as jnp
from jax import lax

CH = 256
FILT = 256
DEPTH = 32
GX = 16
GY = 16
SAMPLES = 4


def block_scale(key, shape, split, smallest, largest):
    def one(axis_at, shards_of):
        steps = jax.random.uniform(jax.random.fold_in(jax.random.fold_in(key, 6), axis_at), (shards_of,), jnp.float32, smallest / len(split), largest / len(split))
        return jnp.repeat(jnp.exp(steps), shape[axis_at] // shards_of).reshape((-1,) + (1,) * (len(shape) - axis_at - 1))

    level = one(*split[0])
    for cut in split[1:]:
        level = level * one(*cut)
    return level


def bell_draw(key, shape, scale, limit, shards=(), dtype=jnp.bfloat16):
    array = scale * jax.random.normal(key, shape, jnp.float32)
    if shards:
        array = array * block_scale(key, shape, shards, -0.22, 0.18)
    return jnp.clip(array, -limit, limit).astype(dtype)


def setup_inputs(seed: int = 0) -> dict:
    splits = jax.random.split(jax.random.key(seed), 5)
    return {
        "features": bell_draw(splits[0], (GX, SAMPLES, GY, DEPTH, CH), 1.0, 6.0, ((0, 4), (1, 2), (2, 4))),
        "kernel": bell_draw(splits[1], (3, 3, 3, CH, FILT), (27 * CH) ** -0.5, 0.078125, ((3, 4), (4, 4))),
        "filter_bias": bell_draw(splits[2], (FILT,), 0.5, 3.0, ((0, 4),)),
        "cotangent": bell_draw(splits[3], (GX, SAMPLES, GY, DEPTH, FILT), 1.0, 6.0, ((0, 4), (1, 2), (4, 4))),
    }


def slope_of(hidden):
    gate = jax.nn.sigmoid(hidden)
    return gate * (1.0 + hidden * (1.0 - gate))


def window_of(padded, first, second, third, rows_x, rows_y, rows_z):
    piece = padded[first:first + rows_x, :, second:second + rows_y, third:third + rows_z, :]
    return piece.reshape(-1, piece.shape[-1])


def reference(features, kernel, filter_bias, cotangent):
    rows_x = features.shape[0]
    count = features.shape[1]
    rows_y = features.shape[2]
    rows_z = features.shape[3]
    channels = features.shape[4]
    filters = kernel.shape[4]
    padded = jnp.pad(features, ((1, 1), (0, 0), (1, 1), (1, 1), (0, 0)))
    hidden = jnp.zeros((rows_x * count * rows_y * rows_z, filters), jnp.float32)
    for first in range(3):
        for second in range(3):
            for third in range(3):
                window = window_of(padded, first, second, third, rows_x, rows_y, rows_z)
                hidden = hidden + jnp.dot(window, kernel[first, second, third], preferred_element_type=jnp.float32)
    hidden = hidden + filter_bias.astype(jnp.float32)[None, :]
    output = jax.nn.silu(hidden).astype(jnp.bfloat16).reshape(rows_x, count, rows_y, rows_z, filters)
    flat_cot = cotangent.reshape(-1, filters).astype(jnp.float32)
    grad_flat = (flat_cot * slope_of(hidden)).astype(jnp.bfloat16)
    grad_pre = grad_flat.reshape(rows_x, count, rows_y, rows_z, filters)
    grad_padded = jnp.pad(grad_pre, ((1, 1), (0, 0), (1, 1), (1, 1), (0, 0)))
    input_grad = jnp.zeros((rows_x * count * rows_y * rows_z, channels), jnp.float32)
    tap_grads = []
    for first in range(3):
        for second in range(3):
            for third in range(3):
                grad_window = window_of(grad_padded, 2 - first, 2 - second, 2 - third, rows_x, rows_y, rows_z)
                input_grad = input_grad + lax.dot_general(grad_window, kernel[first, second, third], (((1,), (1,)), ((), ())), preferred_element_type=jnp.float32)
                window = window_of(padded, first, second, third, rows_x, rows_y, rows_z)
                tap_grads.append(lax.dot_general(window, grad_flat, (((0,), (0,)), ((), ())), preferred_element_type=jnp.float32))
    input_grad = input_grad.astype(jnp.bfloat16).reshape(rows_x, count, rows_y, rows_z, channels)
    kernel_grad = jnp.stack(tap_grads).reshape(3, 3, 3, channels, filters).astype(jnp.float32)
    return output, input_grad, kernel_grad
```

```python
import jax
import jax.numpy as jnp
from jax import lax
from jax.sharding import PartitionSpec as P


def padded(array, axis, dim):
    size, length = lax.axis_size(axis), array.shape[dim]
    up = [(i, i + 1) for i in range(size - 1)]
    down = [(j, i) for i, j in up]
    last = lax.slice_in_dim(array, length - 1, length, axis=dim)
    leading = lax.slice_in_dim(array, 0, 1, axis=dim)
    before = lax.ppermute(last, axis, up)
    after = lax.ppermute(leading, axis, down)
    return jnp.concatenate([before, array, after], axis=dim)


def haloed(array):
    edged = padded(padded(array, "sx", 0), "sy", 2)
    return jnp.pad(edged, ((0, 0), (0, 0), (0, 0), (1, 1), (0, 0)))


def convolve(inputs, weights, layout):
    return lax.conv_general_dilated(
        inputs, weights, (1, 1, 1), ((0, 0),) * 3,
        dimension_numbers=layout, preferred_element_type=jnp.float32)


def local(features, kernel, filter_bias, cotangent):
    rows = kernel.shape[3] // lax.axis_size("sample")
    mine = lax.dynamic_slice_in_dim(kernel, lax.axis_index("sample") * rows, rows, axis=3)
    filts = kernel.shape[4]
    flat = mine.reshape(-1, filts)
    tail = jnp.broadcast_to(filter_bias[None], (16, filts))
    every = lax.all_gather(jnp.concatenate([flat, tail], axis=0), "sy", axis=0, tiled=False)
    bias = every[:, -1].reshape(-1)
    pieces = [every[n, :-16].reshape(mine.shape) for n in range(every.shape[0])]
    wide = jnp.concatenate(pieces, axis=4)
    full = lax.all_gather(wide, ("sx", "sample"), axis=3, tiled=True)
    cot = lax.all_to_all(cotangent, "sy", split_axis=2, concat_axis=4, tiled=True)
    window = haloed(features)
    hidden = convolve(window, full, ("DNHWC", "DHWIO", "DNHWC")) + bias.astype(jnp.float32)
    gate = jax.nn.sigmoid(hidden)
    output = (hidden * gate).astype(jnp.bfloat16)
    grad_pre = (cot.astype(jnp.float32) * (gate * (1.0 + hidden * (1.0 - gate)))).astype(jnp.bfloat16)
    output = lax.all_to_all(output, "sy", split_axis=4, concat_axis=2, tiled=True)
    local_grad = convolve(window, grad_pre, ("DCHWN", "DIHWO", "DHWNC")).astype(jnp.bfloat16)
    part = lax.psum_scatter(local_grad.astype(jnp.bfloat16), ("sx", "sample"), scatter_dimension=3, tiled=True)
    blocks = jnp.stack([part[..., n * filts:(n + 1) * filts] for n in range(lax.axis_size("sy"))])
    blocks = lax.all_to_all(blocks, "sy", split_axis=0, concat_axis=0, tiled=True)
    part = jnp.sum(blocks.astype(jnp.float32), axis=0).astype(jnp.bfloat16).reshape(mine.shape)
    kernel_grad = lax.all_gather(part, "sample", axis=3, tiled=True).astype(jnp.float32)
    input_grad = convolve(haloed(grad_pre), full[::-1, ::-1, ::-1], ("DNHWC", "DHWOI", "DNHWC")).astype(jnp.bfloat16)
    return output, input_grad, kernel_grad


def solution(mesh):
    return jax.shard_map(
        local, mesh=mesh,
        in_specs=(P("sx", "sample", "sy", None, None), P(None, None, None, "sx", "sy"),
                  P("sy"), P("sx", "sample", None, None, "sy")),
        out_specs=(P("sx", "sample", None, None, "sy"), P("sx", "sample", "sy", None, None),
                   P(None, None, None, "sx", "sy")),
        check_vma=False)
```
